32 devices in a mesh: dp: 8 (over z, y), head: 4 (over x, core).
Axes of the slice: x: 2, y: 2, z: 4, core: 2. Of those that a mesh axis runs over, the one named last changes fastest.
Arguments:
- tokens: bfloat16 [5120, 7168], P('dp', 'head'), may hold values from -40 to 40
- query_latent: bfloat16 [5120, 1536], P('dp'), may hold values from -20 to 20
- keyval_latent: bfloat16 [5120, 512], P('dp'), may hold values from -20 to 20
- query_gain: float32 [1536], replicated, may hold values from 0.5 to 12
- keyval_gain: float32 [512], replicated, may hold values from 0.5 to 12
- query_cotangent: bfloat16 [5120, 24576], P('dp', 'head'), may hold values from -20 to 20
- keyval_cotangent: bfloat16 [5120, 32768], P('dp', 'head'), may hold values from -20 to 20
- master_query_up: float32 [1536, 24576], P('dp', 'head'), may hold values from -0.15625 to 0.15625
- master_keyval_up: float32 [512, 32768], P('dp', 'head'), may hold values from -0.25 to 0.25
- master_query_down: float32 [1536, 7168], P('dp', 'head'), may hold values from -0.0625 to 0.0625
- master_keyval_down: float32 [512, 7168], P('dp', 'head'), may hold values from -0.0625 to 0.0625
- mean_query_up: float32 [1536, 24576], P('dp', 'head'), may hold values from -0.15625 to 0.15625
- mean_keyval_up: float32 [512, 32768], P('dp', 'head'), may hold values from -0.15625 to 0.15625
- mean_query_down: float32 [1536, 7168], P('dp', 'head'), may hold values from -0.75 to 0.75
- mean_keyval_down: float32 [512, 7168], P('dp', 'head'), may hold values from -0.75 to 0.75
- square_query_up: float32 [128], P('head'), may hold values from 0.0001 to 0.001
- square_keyval_up: float32 [128], P('head'), may hold values from 0.0001 to 0.001
- square_query_down: float32 [1536], P('dp'), may hold values from 0.003 to 0.1
- square_keyval_down: float32 [512], P('dp'), may hold values from 0.003 to 0.1
Outputs:
- token_grad: bfloat16 [5120, 7168], P('dp', 'head')
- update_query_up: float32 [1536, 24576], P('dp', 'head')
- update_keyval_up: float32 [512, 32768], P('dp', 'head')
- update_query_down: float32 [1536, 7168], P('dp', 'head')
- update_keyval_down: float32 [512, 7168], P('dp', 'head')
- mean_query_up_next: float32 [1536, 24576], P('dp', 'head')
- mean_keyval_up_next: float32 [512, 32768], P('dp', 'head')
- mean_query_down_next: float32 [1536, 7168], P('dp', 'head')
- mean_keyval_down_next: float32 [512, 7168], P('dp', 'head')
- square_query_up_next: float32 [128], P('head')
- square_keyval_up_next: float32 [128], P('head')
- square_query_down_next: float32 [1536], P('dp')
- square_keyval_down_next: float32 [512], P('dp')
The draws below stay inside these ranges and needn't reach their ends.
All inputs are finite; a program needn't handle non-finite values.
Results may differ from the reference program's by a relative error of at most 0.024.
Values may be sent and summed in bfloat16 or wider, within the bound.
No kernel may reach another device: no remote copies, remote signals or barrier semaphores. Data moves between devices by JAX's collectives and lax.ppermute only.
A program may use at most 192 MiB of HBM per device.

```python
import math
import jax
import jax.numpy as jnp
from jax import lax

D = 7168
H = 128
QL = 1536
KVL = 512
QK = 192
KVH = 256
TOK_DEV = 640
TOKENS = 5120
N_DP = 8


def spread_factors(key, count, lower, upper):
    return jnp.exp(jax.random.uniform(key, (count,), jnp.float32, math.log(lower), math.log(upper)))


def rising(count, top):
    return 1.0 + (top - 1.0) * jnp.arange(count, dtype=jnp.float32) / max(count - 1, 1)


def top_factor():
    return 3.0


def drawn_field(keys, rows, cols):
    return jnp.clip(jax.random.normal(keys[1], (rows, cols), jnp.float32), -6.0, 6.0)


def rough_field(key, rows, cols, lower, upper, bound):
    keys = jax.random.split(key, 4)
    column_scale = spread_factors(keys[0], cols, lower, upper)
    values = drawn_field(keys, rows, cols)
    return jnp.clip(values * column_scale[None, :], -bound, bound)


def draw_tokens(key, part):
    field = rough_field(key, TOKENS, D, 0.4, 2.5, 40.0)
    return jnp.clip(field * rising(D, top_factor())[None, :], -40.0, 40.0).astype(jnp.bfloat16)


def draw_query_latent(key, part):
    return rough_field(key, TOKENS, QL, 0.3, 3.0, 20.0).astype(jnp.bfloat16)


def draw_keyval_latent(key, part):
    return rough_field(key, TOKENS, KVL, 0.3, 3.0, 20.0).astype(jnp.bfloat16)


def draw_query_cotangent(key, part):
    return rough_field(key, TOKENS, H * QK, 0.3, 3.0, 20.0).astype(jnp.bfloat16)


def draw_keyval_cotangent(key, part):
    return rough_field(key, TOKENS, H * KVH, 0.3, 3.0, 20.0).astype(jnp.bfloat16)


def draw_query_gain(key, part):
    return spread_factors(key, QL, 0.5, 2.0) * rising(QL, top_factor())


def draw_keyval_gain(key, part):
    return spread_factors(key, KVL, 0.5, 2.0) * rising(KVL, top_factor())


def block_scale(key, extent, cuts, smallest, largest):
    level, own = 1.0, jax.random.fold_in(key, 6)
    for position, blocks in cuts:
        heights = jnp.exp(jax.random.uniform(jax.random.fold_in(own, position), (blocks,), jnp.float32, smallest / len(cuts), largest / len(cuts)))
        level = level * jnp.repeat(heights, extent[position] // blocks).reshape([-1 if axis == position else 1 for axis in range(len(extent))])
    return level


def centred(rng, dims, spread, most, cuts=(), kind=jnp.bfloat16):
    values = spread * jax.random.normal(rng, dims, jnp.float32)
    if cuts:
        values = values * block_scale(rng, dims, cuts, -0.22, 0.18)
    return jnp.clip(values, -most, most).astype(kind)


def setup_inputs(seed: int = 0) -> dict:
    key_of = jax.random.split(jax.random.key(seed), 20)
    return {
        "tokens": draw_tokens(jax.random.fold_in(key_of[19], 71), 0),
        "query_latent": draw_query_latent(jax.random.fold_in(key_of[19], 71), 0),
        "keyval_latent": draw_keyval_latent(jax.random.fold_in(key_of[19], 71), 0),
        "query_gain": draw_query_gain(jax.random.fold_in(key_of[19], 71), 0),
        "keyval_gain": draw_keyval_gain(jax.random.fold_in(key_of[19], 71), 0),
        "query_cotangent": draw_query_cotangent(jax.random.fold_in(key_of[19], 71), 0),
        "keyval_cotangent": draw_keyval_cotangent(jax.random.fold_in(key_of[19], 71), 0),
        "master_query_up": centred(key_of[7], (QL, H * QK), QL ** -0.5, 0.15625, ((0, 8), (1, 4)), jnp.float32),
        "master_keyval_up": centred(key_of[8], (KVL, H * KVH), KVL ** -0.5, 0.25, ((0, 8), (1, 4)), jnp.float32),
        "master_query_down": centred(key_of[9], (QL, D), D ** -0.5, 0.0625, ((0, 8), (1, 4)), jnp.float32),
        "master_keyval_down": centred(key_of[10], (KVL, D), D ** -0.5, 0.0625, ((0, 8), (1, 4)), jnp.float32),
        "mean_query_up": centred(key_of[11], (QL, H * QK), 0.01, 0.15625, ((0, 8), (1, 4)), jnp.float32),
        "mean_keyval_up": centred(key_of[12], (KVL, H * KVH), 0.01, 0.15625, ((0, 8), (1, 4)), jnp.float32),
        "mean_query_down": centred(key_of[13], (QL, D), 0.05, 0.75, ((0, 8), (1, 4)), jnp.float32),
        "mean_keyval_down": centred(key_of[14], (KVL, D), 0.05, 0.75, ((0, 8), (1, 4)), jnp.float32),
        "square_query_up": jnp.clip(jnp.exp(math.log(0.001) - 2.3025852 * jax.random.uniform(key_of[15], (H,), jnp.float32) ** block_scale(key_of[15], (H,), ((0, 4),), -0.2, 0.2)), 0.0001, 0.001),
        "square_keyval_up": jnp.clip(jnp.exp(math.log(0.001) - 2.3025852 * jax.random.uniform(key_of[16], (H,), jnp.float32) ** block_scale(key_of[16], (H,), ((0, 4),), -0.2, 0.2)), 0.0001, 0.001),
        "square_query_down": jnp.clip(jnp.exp(math.log(0.1) - 3.506558 * jax.random.uniform(key_of[17], (QL,), jnp.float32) ** block_scale(key_of[17], (QL,), ((0, 8),), -0.2, 0.2)), 0.003, 0.1),
        "square_keyval_down": jnp.clip(jnp.exp(math.log(0.1) - 3.506558 * jax.random.uniform(key_of[18], (KVL,), jnp.float32) ** block_scale(key_of[18], (KVL,), ((0, 8),), -0.2, 0.2)), 0.003, 0.1),
    }


norm_eps = 1e-06
adam_eps = 1e-08
beta_first = 0.9
beta_second = 0.95
adam_step = 10

def normalize(latent, gain):
    values = latent.astype(jnp.float32)
    inverse = lax.rsqrt(lax.optimization_barrier(jnp.mean(values * values, axis=1, keepdims=True)) + norm_eps)
    normed = (values * inverse * gain).astype(jnp.bfloat16)
    return (values, inverse, normed)

def norm_back(values, inverse, gain, upstream):
    weighted = gain * upstream
    inner = lax.optimization_barrier(jnp.sum(values * weighted, axis=1, keepdims=True)) / values.shape[1]
    return (inverse * weighted - values * inverse ** 3 * inner).astype(jnp.bfloat16)

def group_grad(left, right):
    left_groups = left.reshape(N_DP, TOK_DEV, left.shape[1])
    right_groups = right.reshape(N_DP, TOK_DEV, right.shape[1])

    def accumulate(total, pair):
        partial_sum = jnp.dot(pair[0].T, pair[1], preferred_element_type=jnp.float32)
        rounded = lax.optimization_barrier(partial_sum.astype(jnp.bfloat16))
        return (total + rounded.astype(jnp.float32), None)
    start = jnp.zeros((left.shape[1], right.shape[1]), jnp.float32)
    total, _ = lax.scan(accumulate, start, (left_groups, right_groups))
    return total / TOKENS

def direction(first_next, second_wide):
    first_scale = 1.0 - beta_first ** adam_step
    second_scale = 1.0 - beta_second ** adam_step
    return first_next / first_scale / (jnp.sqrt(second_wide / second_scale) + adam_eps)

def reference(tokens, query_latent, keyval_latent, query_gain, keyval_gain, query_cotangent, keyval_cotangent, master_query_up, master_keyval_up, master_query_down, master_keyval_down, mean_query_up, mean_keyval_up, mean_query_down, mean_keyval_down, square_query_up, square_keyval_up, square_query_down, square_keyval_down):
    query_up = master_query_up.astype(jnp.bfloat16)
    keyval_up = master_keyval_up.astype(jnp.bfloat16)
    query_down = master_query_down.astype(jnp.bfloat16)
    keyval_down = master_keyval_down.astype(jnp.bfloat16)
    query_values, query_inverse, query_normed = normalize(query_latent, query_gain)
    keyval_values, keyval_inverse, keyval_normed = normalize(keyval_latent, keyval_gain)
    query_upstream = jnp.dot(query_cotangent, query_up.T, preferred_element_type=jnp.float32)
    keyval_upstream = jnp.dot(keyval_cotangent, keyval_up.T, preferred_element_type=jnp.float32)
    query_slope = norm_back(query_values, query_inverse, query_gain, query_upstream)
    keyval_slope = norm_back(keyval_values, keyval_inverse, keyval_gain, keyval_upstream)
    token_grad = (jnp.dot(query_slope, query_down, preferred_element_type=jnp.float32) + jnp.dot(keyval_slope, keyval_down, preferred_element_type=jnp.float32)).astype(jnp.bfloat16)
    grad_query_up = group_grad(query_normed, query_cotangent)
    grad_keyval_up = group_grad(keyval_normed, keyval_cotangent)
    grad_query_down = group_grad(query_slope, tokens)
    grad_keyval_down = group_grad(keyval_slope, tokens)
    mean_query_up_next = beta_first * mean_query_up + (1.0 - beta_first) * grad_query_up
    mean_keyval_up_next = beta_first * mean_keyval_up + (1.0 - beta_first) * grad_keyval_up
    mean_query_down_next = beta_first * mean_query_down + (1.0 - beta_first) * grad_query_down
    mean_keyval_down_next = beta_first * mean_keyval_down + (1.0 - beta_first) * grad_keyval_down
    head_query = lax.optimization_barrier(jnp.mean((grad_query_up * grad_query_up).reshape(QL, H, QK), axis=(0, 2)))
    head_keyval = lax.optimization_barrier(jnp.mean((grad_keyval_up * grad_keyval_up).reshape(KVL, H, KVH), axis=(0, 2)))
    row_query = lax.optimization_barrier(jnp.mean(grad_query_down * grad_query_down, axis=1))
    row_keyval = lax.optimization_barrier(jnp.mean(grad_keyval_down * grad_keyval_down, axis=1))
    square_query_up_next = beta_second * square_query_up + (1.0 - beta_second) * head_query
    square_keyval_up_next = beta_second * square_keyval_up + (1.0 - beta_second) * head_keyval
    square_query_down_next = beta_second * square_query_down + (1.0 - beta_second) * row_query
    square_keyval_down_next = beta_second * square_keyval_down + (1.0 - beta_second) * row_keyval
    update_query_up = direction(mean_query_up_next, jnp.repeat(square_query_up_next, QK)[None, :])
    update_keyval_up = direction(mean_keyval_up_next, jnp.repeat(square_keyval_up_next, KVH)[None, :])
    update_query_down = direction(mean_query_down_next, square_query_down_next[:, None])
    update_keyval_down = direction(mean_keyval_down_next, square_keyval_down_next[:, None])
    return (token_grad, update_query_up, update_keyval_up, update_query_down, update_keyval_down, mean_query_up_next, mean_keyval_up_next, mean_query_down_next, mean_keyval_down_next, square_query_up_next, square_keyval_up_next, square_query_down_next, square_keyval_down_next)
```

```python
import jax
import jax.numpy as jnp
from jax import lax
from jax.sharding import Mesh, PartitionSpec as P

D = 7168
QL = 1536
KVL = 512
QK = 192
KVH = 256


norm_eps = 1e-06
adam_eps = 1e-08
beta_first = 0.9
beta_second = 0.95
adam_step = 10


LINE, PAIR, WIDE, CORE = "line", "pair", "wide", "core"
SWAP = [(0, 1), (1, 0)]
bf16 = jnp.bfloat16
f32 = jnp.float32


def rows_product(left, right):
    return lax.dot_general(left, right, (((0,), (0,)), ((), ())), preferred_element_type=f32)


def cols_product(left, right):
    return lax.dot_general(left, right, (((1,), (1,)), ((), ())), preferred_element_type=f32)


def direction(first_next, second_wide):
    first_scale = 1.0 - beta_first**adam_step
    second_scale = 1.0 - beta_second**adam_step
    return first_next / first_scale / (jnp.sqrt(second_wide / second_scale) + adam_eps)


def moment_first(first, grad):
    return beta_first * first + (1.0 - beta_first) * grad


def moment_second(second, block_mean):
    return beta_second * second + (1.0 - beta_second) * block_mean


def after(value, *others):
    return lax.optimization_barrier((value, *others))[0]


def swap(value, axis):
    return lax.ppermute(value, axis, SWAP)


def half(value, index, dim):
    size = value.shape[dim] // 2
    return lax.dynamic_slice_in_dim(value, index * size, size, dim)


def in_order(index, own, other, dim):
    return jnp.where(
        index == 0,
        jnp.concatenate([own, other], dim),
        jnp.concatenate([other, own], dim),
    )


def rotated(value, dim, place, count):
    size = value.shape[dim] // count
    return jnp.concatenate(
        [
            lax.dynamic_slice_in_dim(value, ((place - m) % count) * size, size, dim)
            for m in range(count)
        ],
        dim,
    )


def line_gather(own, count, first=None):
    right, left, steps = [], [], []
    going_right = going_left = own
    for s in range(count - 1):
        going_right = lax.ppermute(going_right, LINE, [(i, i + 1) for i in range(s, count - 1)])
        going_left = lax.ppermute(going_left, LINE, [(i, i - 1) for i in range(1, count - s)])
        right.append(going_right)
        left.append(going_left)
    blocks = [own] + [right[s] + left[count - 2 - s] for s in range(count - 1)]
    return blocks, list(zip(right, left))


def line_scatter(blocks, count):
    right = left = None
    steps = []
    for s in range(count - 1):
        send_right = blocks[(s + 1) % count]
        send_left = blocks[count - 1 - s]
        if s:
            send_right = (send_right.astype(f32) + right.astype(f32)).astype(bf16)
            send_left = (send_left.astype(f32) + left.astype(f32)).astype(bf16)
        right = lax.ppermute(send_right, LINE, [(i, i + 1) for i in range(s + 1)])
        left = lax.ppermute(send_left, LINE, [(count - 1 - i, count - 2 - i) for i in range(s + 1)])
        steps.append((right, left))
    total = blocks[0].astype(f32) + right.astype(f32) + left.astype(f32)
    return total, steps


def head_gather(piece, wides, wide, core):
    rows, cols = piece.shape
    if wides != 2:
        return lax.all_gather(piece, (WIDE, CORE), axis=0, tiled=True)
    both = in_order(wide, piece, swap(piece, WIDE), 0).reshape(2, 1, rows, cols)
    other = swap(both, CORE)
    return in_order(core, both, other, 1).reshape(4 * rows, cols)


def head_scatter(partial, wides, wide, core):
    _, tokens, cols = partial.shape
    rows = tokens // (wides * 2)
    view = partial.astype(bf16).reshape(2, wides, 2, rows, cols)
    keep = lax.dynamic_index_in_dim(view, core, 2, keepdims=False)
    send = lax.dynamic_index_in_dim(view, 1 - core, 2, keepdims=False)
    view = keep.astype(f32) + swap(send, CORE).astype(f32)
    if wides == 2:
        keep = lax.dynamic_index_in_dim(view, wide, 1, keepdims=False)
        send = lax.dynamic_index_in_dim(view, 1 - wide, 1, keepdims=False).astype(bf16)
        view = keep + swap(send, WIDE).astype(f32)
    else:
        view = lax.psum_scatter(view.astype(bf16), WIDE, scatter_dimension=1, tiled=False).astype(f32)
    return view[0] + swap(view[1].astype(bf16), PAIR).astype(f32)


def local(
    tokens,
    query_latent,
    keyval_latent,
    query_gain,
    keyval_gain,
    query_cotangent,
    keyval_cotangent,
    master_query_up,
    master_keyval_up,
    master_query_down,
    master_keyval_down,
    mean_query_up,
    mean_keyval_up,
    mean_query_down,
    mean_keyval_down,
    square_query_up,
    square_keyval_up,
    square_query_down,
    square_keyval_down,
):
    count, wides = lax.axis_size(LINE), lax.axis_size(WIDE)
    place, side = lax.axis_index(LINE), lax.axis_index(PAIR)
    wide, core = lax.axis_index(WIDE), lax.axis_index(CORE)
    token_count = tokens.shape[0] * count * 2
    blocks_dp = count * 2
    rows_q, rows_kv = master_query_up.shape[0], master_keyval_up.shape[0]
    share = tokens.shape[0] // (wides * 2)
    start = (wide * 2 + core) * share

    def pair_rows(master, gate):
        low = master.astype(bf16)
        sent = half(low, 1 - side, 1)
        if gate is not None:
            sent = after(sent, gate)
        other = swap(sent, PAIR)
        return in_order(side, half(low, side, 1), other, 0), other

    pair_q, came_q = pair_rows(master_query_up, None)
    pair_kv, came_kv = pair_rows(master_keyval_up, came_q)

    latent = jnp.concatenate(
        [rotated(query_latent, 1, place, count), rotated(keyval_latent, 1, place, count)], 1
    )
    gain_q, gain_kv = rotated(query_gain, 0, place, count), rotated(keyval_gain, 0, place, count)
    own_piece = lax.dynamic_slice_in_dim(latent, start, share, 0)
    other_piece = swap(after(own_piece, came_q), PAIR)
    other_latent = head_gather(other_piece, wides, wide, core)
    both_latent = jnp.concatenate([latent, other_latent], 0)

    def normalize(values, gain):
        values = values.astype(f32)
        inverse = lax.rsqrt(jnp.mean(values * values, axis=1, keepdims=True) + norm_eps)
        return (values * inverse * gain).astype(bf16)

    normed_q = normalize(both_latent[:, :QL], gain_q)
    normed_kv = normalize(both_latent[:, QL:], gain_kv)

    cot_q_other = swap(after(half(query_cotangent, 1 - side, 1), came_kv), PAIR)
    cot_kv_other = swap(after(half(keyval_cotangent, 1 - side, 1), cot_q_other), PAIR)
    cot_q = jnp.concatenate([half(query_cotangent, side, 1), cot_q_other], 0)
    cot_kv = jnp.concatenate([half(keyval_cotangent, side, 1), cot_kv_other], 0)

    whole_q, steps_q = line_gather(pair_q, count)
    whole_kv, steps_kv = line_gather(after(pair_kv, *steps_q[-2]), count)

    shard_down = jnp.concatenate([master_query_down, master_keyval_down], 0).astype(bf16)
    rows_down = rows_q + rows_kv
    other_down = swap(after(shard_down, cot_q_other), PAIR)
    pair_down = in_order(side, shard_down, other_down, 0)
    whole_down, _ = line_gather(after(pair_down, *steps_kv[-2]), count)

    def up_grad(normed, cot, gate):
        part = rows_product(normed, cot).astype(bf16)
        size = part.shape[0] // count
        blocks = [part[m * size : (m + 1) * size] for m in range(count)]
        if gate is not None:
            blocks = list(lax.optimization_barrier((*blocks, *gate))[:count])
        total, steps = line_scatter(blocks, count)
        mine = half(total, side, 0)
        other = swap(half(total, 1 - side, 0).astype(bf16), PAIR).astype(f32)
        return in_order(side, mine, other, 1) / token_count, steps

    grad_query_up, scatter_q = up_grad(normed_q, cot_q, None)
    grad_keyval_up, _ = up_grad(normed_kv, cot_kv, scatter_q[-2])

    def upstream(cot, whole):
        partial = cols_product(cot, jnp.concatenate(whole, 0)).astype(bf16)
        partial = partial.reshape(2, partial.shape[0] // 2, partial.shape[1])
        return head_scatter(partial, wides, wide, core)

    def norm_back(values, gain, share_up):
        values = values.astype(f32)
        inverse = lax.rsqrt(jnp.mean(values * values, axis=1, keepdims=True) + norm_eps)
        weighted = gain * share_up
        inner = jnp.sum(values * weighted, axis=1, keepdims=True) / values.shape[1]
        return (inverse * weighted - values * inverse**3 * inner).astype(bf16)

    piece_q = norm_back(own_piece[:, :QL], gain_q, upstream(cot_q, whole_q))
    piece_kv = norm_back(own_piece[:, QL:], gain_kv, upstream(cot_kv, whole_kv))
    piece = jnp.concatenate(
        [
            piece_q.reshape(share, blocks_dp, rows_q),
            piece_kv.reshape(share, blocks_dp, rows_kv),
        ],
        2,
    ).reshape(share, blocks_dp * rows_down)
    slope = head_gather(piece, wides, wide, core)

    token_grad = jnp.dot(
        slope, jnp.concatenate(whole_down, 0), preferred_element_type=f32
    ).astype(bf16)

    part_down = rows_product(slope, tokens).astype(bf16)
    width = part_down.shape[1]
    cut = width * 5 // 8 // 128 * 128
    part_down = part_down.reshape(count, 2, rows_down, width)
    near, far = part_down[..., :cut], part_down[..., cut:]
    keep = lax.dynamic_index_in_dim(near, side, 1, keepdims=False)
    send = lax.dynamic_index_in_dim(near, 1 - side, 1, keepdims=False)
    near = (keep.astype(f32) + swap(send, PAIR).astype(f32)).astype(bf16)
    near, _ = line_scatter([near[m] for m in range(count)], count)
    far, _ = line_scatter([far[m] for m in range(count)], count)
    keep = lax.dynamic_index_in_dim(far, side, 0, keepdims=False)
    send = lax.dynamic_index_in_dim(far, 1 - side, 0, keepdims=False).astype(bf16)
    far = keep + swap(send, PAIR).astype(f32)
    grad_down = jnp.concatenate([near, far], 1) / token_count
    grad_query_down, grad_keyval_down = grad_down[:rows_q], grad_down[rows_q:]

    local_heads = grad_query_up.shape[1] // QK
    head_query = jnp.sum(
        (grad_query_up * grad_query_up).reshape(rows_q, local_heads, QK), axis=(0, 2)
    )
    head_keyval = jnp.sum(
        (grad_keyval_up * grad_keyval_up).reshape(rows_kv, local_heads, KVH), axis=(0, 2)
    )
    row_query = jnp.sum(grad_query_down * grad_query_down, axis=1)
    row_keyval = jnp.sum(grad_keyval_down * grad_keyval_down, axis=1)
    head_query, head_keyval = lax.psum((head_query, head_keyval), (LINE, PAIR))
    row_query, row_keyval = lax.psum((row_query, row_keyval), (WIDE, CORE))
    square_query_up_next = moment_second(square_query_up, head_query / (QL * QK))
    square_keyval_up_next = moment_second(square_keyval_up, head_keyval / (KVL * KVH))
    square_query_down_next = moment_second(square_query_down, row_query / D)
    square_keyval_down_next = moment_second(square_keyval_down, row_keyval / D)
    mean_query_up_next = moment_first(mean_query_up, grad_query_up)
    mean_keyval_up_next = moment_first(mean_keyval_up, grad_keyval_up)
    mean_query_down_next = moment_first(mean_query_down, grad_query_down)
    mean_keyval_down_next = moment_first(mean_keyval_down, grad_keyval_down)
    update_query_up = direction(mean_query_up_next, jnp.repeat(square_query_up_next, QK)[None, :])
    update_keyval_up = direction(
        mean_keyval_up_next, jnp.repeat(square_keyval_up_next, KVH)[None, :]
    )
    update_query_down = direction(mean_query_down_next, square_query_down_next[:, None])
    update_keyval_down = direction(mean_keyval_down_next, square_keyval_down_next[:, None])
    return (
        token_grad,
        update_query_up,
        update_keyval_up,
        update_query_down,
        update_keyval_down,
        mean_query_up_next,
        mean_keyval_up_next,
        mean_query_down_next,
        mean_keyval_down_next,
        square_query_up_next,
        square_keyval_up_next,
        square_query_down_next,
        square_keyval_down_next,
    )


def solution(mesh):
    data, heads = mesh.devices.shape
    grid = Mesh(mesh.devices.reshape(data // 2, 2, heads // 2, 2), (LINE, PAIR, WIDE, CORE))
    dp, head = (LINE, PAIR), (WIDE, CORE)
    both, rows = P(dp, head), P(dp, None)
    return jax.shard_map(
        local,
        mesh=grid,
        in_specs=(both, rows, rows, P(), P())
        + (both,) * 10
        + (P(head), P(head), P(dp), P(dp)),
        out_specs=(both,) * 9 + (P(head), P(head), P(dp), P(dp)),
        check_vma=False,
    )
```
